128 devices in a mesh: req: 16 (over x, z), tile: 8 (over y, core).
Axes of the slice: x: 4, y: 4, z: 4, core: 2. Of those that a mesh axis runs over, the one named last changes fastest.
Arguments:
- latents: bfloat16 [1024, 16, 128], P(('req', 'tile')), may hold values from -6 to 6
- piece_dest: int32 [1024], replicated, may hold values from 0 to 1023, as said below
- frames: int32 [16], replicated, may hold values from 1 to 2
- heights: int32 [16], replicated, may hold values from 16 to 32
- widths: int32 [16], replicated, may hold values from 64 to 128
- w_in: bfloat16 [3, 3, 3, 384, 16], replicated, may hold values from -0.3125 to 0.3125
- b_in: float32 [384], replicated, may hold values from -3 to 3
- gain_norm: float32 [384], replicated, may hold values from 0.5 to 1.5
- w_res: bfloat16 [3, 3, 3, 384, 384], replicated, may hold values from -0.0625 to 0.0625
- b_res: float32 [384], replicated, may hold values from -3 to 3
- w_time: bfloat16 [3, 768, 384], replicated, may hold values from -0.1875 to 0.1875
- b_time: float32 [768], replicated, may hold values from -3 to 3
- w_up: bfloat16 [3, 3, 192, 384], replicated, may hold values from -0.109375 to 0.109375
- b_up: float32 [192], replicated, may hold values from -3 to 3
Outputs:
- decoded: bfloat16 [16, 192, 4, 64, 256], P('req', None, None, 'tile')
The draws below stay inside these ranges and needn't reach their ends.
Inputs may be any that keep to these rules, and one draw needn't show every extreme that they name: piece_dest is a permutation of the decoder slots. Requests are packed one after another in a drawn order, each request's rows frame after frame and row after row, so the 8 rows of one device are consecutive rows of one request and no device sends more than 4 rows to one device.
All inputs are finite; a program needn't handle non-finite values.
Results may differ from the reference program's by a relative error of at most 0.0075.
Values may be sent and summed in bfloat16 or wider, within the bound.
No kernel may reach another device: no remote copies, remote signals or barrier semaphores. Data moves between devices by JAX's collectives and lax.ppermute only.
A program may use at most 192 MiB of HBM per device.

```python
import jax
import jax.numpy as jnp
from jax import lax

C_LAT = 16
C_MID = 384
C_OUT = 192
LFRAMES = 2
LROWS = 4
LCOLS = 128
SLOTS = 8
PIECES = 1024
GROUPS = 16
HL = 32
N_TILE = 8


def draw_piece_dest(key, part):
    packed_order = jax.random.permutation(key, GROUPS).astype(jnp.int32)
    positions = jnp.arange(PIECES, dtype=jnp.int32)
    request_slot = positions // (LFRAMES * HL)
    within = positions % (LFRAMES * HL)
    frame_id = within // HL
    row_id = within % HL
    group_id = packed_order[request_slot]
    tile_id = row_id // LROWS
    local_row = row_id % LROWS
    return ((group_id * N_TILE + tile_id) * SLOTS + frame_id * LROWS + local_row).astype(jnp.int32)


def touch_ends(drawn, rng, low, high):
    dims = drawn.shape
    place = [jax.random.randint(jax.random.fold_in(rng, axis), (), 0, dims[axis]) for axis in range(len(dims))]
    drawn = drawn.at[tuple(place)].set(low)
    longest = dims.index(max(dims))
    place[longest] = (place[longest] + 1) % dims[longest]
    return drawn.at[tuple(place)].set(high)


def levels(stream_key, extent, split, low, high):
    def one(axis_at, shards_of):
        draws = jax.random.uniform(jax.random.fold_in(jax.random.fold_in(stream_key, 6), axis_at), (shards_of,), jnp.float32, low / len(split), high / len(split))
        return jnp.repeat(jnp.exp(draws), extent[axis_at] // shards_of).reshape((-1,) + (1,) * (len(extent) - axis_at - 1))

    factor_of = one(*split[0])
    for cut in split[1:]:
        factor_of = factor_of * one(*cut)
    return factor_of


def gaussian(stream_key, shape, width, reach, pieces=(), kind=jnp.bfloat16):
    array = width * jax.random.normal(stream_key, shape, jnp.float32)
    if pieces:
        array = array * levels(stream_key, shape, pieces, -0.22, 0.18)
    return jnp.clip(array, -reach, reach).astype(kind)


def setup_inputs(seed: int = 0) -> dict:
    keys = jax.random.split(jax.random.key(seed), 15)
    return {
        "latents": gaussian(keys[0], (PIECES, C_LAT, LCOLS), 1.0, 6.0, ((0, 128),)),
        "piece_dest": draw_piece_dest(jax.random.fold_in(keys[14], 71), 0),
        "frames": touch_ends(jax.random.randint(keys[2], (GROUPS,), 1, LFRAMES + 1), jax.random.fold_in(keys[2], 1), 1, LFRAMES).astype(jnp.int32),
        "heights": touch_ends(jax.random.randint(keys[3], (GROUPS,), HL // 2, HL + 1), jax.random.fold_in(keys[3], 1), HL // 2, HL).astype(jnp.int32),
        "widths": touch_ends(jax.random.randint(keys[4], (GROUPS,), LCOLS // 2, LCOLS + 1), jax.random.fold_in(keys[4], 1), LCOLS // 2, LCOLS).astype(jnp.int32),
        "w_in": gaussian(keys[5], (3, 3, 3, C_MID, C_LAT), (27 * C_LAT) ** -0.5, 0.3125),
        "b_in": gaussian(keys[6], (C_MID,), 0.5, 3.0, (), jnp.float32),
        "gain_norm": jnp.clip(1.0 + 0.1 * jax.random.normal(keys[7], (C_MID,), jnp.float32), 0.5, 1.5),
        "w_res": gaussian(keys[8], (3, 3, 3, C_MID, C_MID), (27 * C_MID) ** -0.5, 0.0625),
        "b_res": gaussian(keys[9], (C_MID,), 0.5, 3.0, (), jnp.float32),
        "w_time": gaussian(keys[10], (3, 2 * C_MID, C_MID), (3 * C_MID) ** -0.5, 0.1875),
        "b_time": gaussian(keys[11], (2 * C_MID,), 0.5, 3.0, (), jnp.float32),
        "w_up": gaussian(keys[12], (3, 3, C_OUT, C_MID), (9 * C_MID) ** -0.5, 0.109375),
        "b_up": gaussian(keys[13], (C_OUT,), 0.5, 3.0, (), jnp.float32),
    }


def causal_conv(inputs, weight, offsets):
    frame_count, row_count, col_count = inputs.shape[1:]
    padded = jnp.pad(inputs, ((0, 0), (2, 0), (1, 1), (1, 1)))
    summed = jnp.zeros((weight.shape[3], frame_count, row_count, col_count), jnp.float32)
    for tap_t in range(3):
        for tap_r in range(3):
            for tap_c in range(3):
                summed = summed + jnp.einsum('oc,cthw->othw', weight[tap_t, tap_r, tap_c].astype(jnp.float32), padded[:, tap_t:tap_t + frame_count, tap_r:tap_r + row_count, tap_c:tap_c + col_count], precision=lax.Precision.HIGHEST)
    return summed + offsets[:, None, None, None]

def reference(latents, piece_dest, frames, heights, widths, w_in, b_in, gain_norm, w_res, b_res, w_time, b_time, w_up, b_up):
    arranged = jnp.zeros((PIECES, C_LAT, LCOLS), jnp.bfloat16).at[piece_dest].set(latents)
    latent_grid = arranged.reshape(GROUPS, N_TILE, LFRAMES, LROWS, C_LAT, LCOLS)
    latent_grid = latent_grid.transpose(0, 4, 2, 1, 3, 5).reshape(GROUPS, C_LAT, LFRAMES, HL, LCOLS)

    def decode_one(items):
        request_grid, frame_limit, row_limit, col_limit = items
        frame_ids = jnp.arange(LFRAMES, dtype=jnp.int32)
        row_ids = jnp.arange(HL, dtype=jnp.int32)
        col_ids = jnp.arange(LCOLS, dtype=jnp.int32)
        region = ((frame_ids < frame_limit)[:, None, None] & (row_ids < row_limit)[None, :, None] & (col_ids < col_limit)[None, None, :]).astype(jnp.float32)
        masked = (request_grid.astype(jnp.float32) * region).astype(jnp.bfloat16)
        first = causal_conv(masked.astype(jnp.float32), w_in, b_in).astype(jnp.bfloat16)
        first_f = first.astype(jnp.float32)
        scaled = first_f * lax.rsqrt(lax.optimization_barrier(jnp.mean(first_f * first_f, axis=0, keepdims=True)) + 1e-06) * gain_norm[:, None, None, None]
        normed = (jax.nn.silu(scaled) * region).astype(jnp.bfloat16)
        block = (first_f + causal_conv(normed.astype(jnp.float32), w_res, b_res)).astype(jnp.bfloat16)
        padded = jnp.pad(block.astype(jnp.float32), ((0, 0), (2, 0), (0, 0), (0, 0)))
        twice = jnp.zeros((2 * C_MID, LFRAMES, HL, LCOLS), jnp.float32)
        for tap_t in range(3):
            twice = twice + jnp.einsum('oc,cthw->othw', w_time[tap_t].astype(jnp.float32), padded[:, tap_t:tap_t + LFRAMES], precision=lax.Precision.HIGHEST)
        twice = twice + b_time[:, None, None, None]
        doubled = jnp.stack([twice[:C_MID], twice[C_MID:]], axis=2).reshape(C_MID, 2 * LFRAMES, HL, LCOLS)
        time_region = jnp.repeat(region, 2, axis=0)
        timed = (doubled * time_region).astype(jnp.bfloat16)
        widened = jnp.repeat(jnp.repeat(timed.astype(jnp.float32), 2, axis=2), 2, axis=3)
        padded_up = jnp.pad(widened, ((0, 0), (0, 0), (1, 1), (1, 1)))
        summed = jnp.zeros((C_OUT, 2 * LFRAMES, 2 * HL, 2 * LCOLS), jnp.float32)
        for tap_r in range(3):
            for tap_c in range(3):
                summed = summed + jnp.einsum('oc,cthw->othw', w_up[tap_r, tap_c].astype(jnp.float32), padded_up[:, :, tap_r:tap_r + 2 * HL, tap_c:tap_c + 2 * LCOLS], precision=lax.Precision.HIGHEST)
        summed = summed + b_up[:, None, None, None]
        out_region = jnp.repeat(jnp.repeat(time_region, 2, axis=1), 2, axis=2)
        return (summed * out_region).astype(jnp.bfloat16)
    return lax.map(decode_one, (latent_grid, frames, heights, widths))
```

```python
import functools

import jax
import jax.numpy as jnp
from jax import lax
from jax.experimental import pallas as pl
from jax.experimental.pallas import tpu as pltpu
from jax.sharding import PartitionSpec as P

LAT = 16
MID = 384
OUT = 192
FRAMES = 2
ROWS = 4
COLS = 128
BF = jnp.bfloat16
F32 = jnp.float32


def taps_of(frame):
    return [(tap, frame - 2 + tap) for tap in range(3) if frame - 2 + tap >= 0]


def column(vec_ref):
    return jnp.transpose(jnp.broadcast_to(vec_ref[...], (COLS, vec_ref.shape[1])))


def shifts(x):
    col = lax.broadcasted_iota(jnp.int32, x.shape, 1)
    before = jnp.where(col == 0, 0.0, pltpu.roll(x, 1, 1))
    after = jnp.where(col == COLS - 1, 0.0, pltpu.roll(x, COLS - 1, 1))
    return before, x, after


def decode_kernel(
    info,
    rim_a,
    rim_b,
    rim_c,
    rim_d,
    b_in,
    gain,
    b_res,
    b_time,
    b_up,
    w_in_hbm,
    w_res_hbm,
    w_time_hbm,
    w_up_hbm,
    out_hbm,
    w_in,
    w_res,
    w_time,
    w_up,
    lat_cols,
    conv,
    first,
    norm_cols,
    block,
    time_cols,
    w_phase,
    bias_mid,
    bias_time,
    bias_up,
    spread,
    tall,
    out_buf,
    in_sems,
    out_sems,
):
    loads = [
        pltpu.make_async_copy(w_in_hbm, w_in, in_sems.at[0]),
        pltpu.make_async_copy(w_up_hbm, w_up, in_sems.at[1]),
        pltpu.make_async_copy(w_res_hbm.at[pl.ds(9, 18)], w_res, in_sems.at[2]),
        pltpu.make_async_copy(w_time_hbm.at[pl.ds(1, 2)], w_time, in_sems.at[3]),
    ]
    for load in loads:
        load.start()
    odd = info[0] == 1
    frame_limit, row_limit, col_limit, row_base = info[1], info[2], info[3], info[4]
    cols = lax.broadcasted_iota(jnp.int32, (1, COLS), 1)
    col_mask = (cols < col_limit).astype(F32)

    def mask_at(frame, row):
        inside = (frame < frame_limit) & (row >= 0) & (row < row_limit)
        return col_mask * jnp.where(inside, 1.0, 0.0).astype(F32)

    bias_mid[0] = column(b_in)
    bias_mid[1] = column(gain)
    bias_mid[2] = column(b_res)
    bias_time[...] = column(b_time)
    bias_up[...] = column(b_up)
    key = lax.broadcasted_iota(jnp.int32, (2 * COLS, 2 * COLS), 0)
    place = lax.broadcasted_iota(jnp.int32, (2 * COLS, 2 * COLS), 1)
    spread[...] = (key == (place % 2) * COLS + place // 2).astype(F32).astype(BF)

    for frame in range(FRAMES):
        main_even, main_odd = (rim_a, rim_b) if frame == 0 else (rim_b, rim_a)
        rest_even, rest_odd = (rim_d, rim_c) if frame == 0 else (rim_c, rim_d)
        for row in range(10):
            even = rest_even[row] if row < 3 else main_even[row - 3]
            other = main_odd[row] if row < 7 else rest_odd[row - 7]
            value = jnp.where(odd, other.astype(F32), even.astype(F32))
            value = value * mask_at(frame, row_base - 3 + row)
            for at, moved in enumerate(shifts(value)):
                lat_cols[frame, row, pl.ds(at * LAT, LAT), :] = moved.astype(BF)

    loads[0].wait()
    for frame in range(FRAMES):
        taps = taps_of(frame)
        weight = w_in[pl.ds(taps[0][0] * 9 * LAT, len(taps) * 9 * LAT), :]
        pieces = []
        for row in range(8):
            pieces.append(
                jnp.concatenate(
                    [lat_cols[src, row + d] for _, src in taps for d in range(3)], axis=0
                )
            )
        data = jnp.concatenate(pieces, axis=1)
        summed = lax.dot_general(
            weight, data, (((0,), (0,)), ((), ())), preferred_element_type=F32
        )
        for row in range(8):
            conv[frame * 8 + row] = summed[:, row * COLS : (row + 1) * COLS]

    def norm_row(at, carry):
        frame, row = at // 8, at % 8
        value = (conv[at] + bias_mid[0]).astype(BF)
        first[at] = value
        value = value.astype(F32)
        mean = jnp.sum(value * value, axis=0, keepdims=True) * (1.0 / MID)
        scaled = value * lax.rsqrt(mean + 1e-6) * bias_mid[1]
        normed = scaled / (1.0 + jnp.exp(-scaled)) * mask_at(frame, row_base - 2 + row)
        for tap, moved in enumerate(shifts(normed)):
            norm_cols[at, pl.ds(tap * MID, MID), :] = moved.astype(BF)
        return carry

    lax.fori_loop(0, FRAMES * 8, norm_row, 0)

    loads[1].wait()

    def two(phase, taps):
        return (taps[0], taps[1] + taps[2]) if phase == 0 else (taps[0] + taps[1], taps[2])

    def combine(at, carry):
        base = pl.multiple_of(at * 16, 16)
        whole = [
            [w_up[3 * d + e, pl.ds(base, 16), :].astype(F32) for e in range(3)] for d in range(3)
        ]
        for pr in range(2):
            rows = [two(pr, [whole[d][e] for d in range(3)]) for e in range(3)]
            for dr in range(2):
                for pc in range(2):
                    cells = two(pc, [rows[e][dr] for e in range(3)])
                    for dc in range(2):
                        w_phase[2 * pr + pc, pl.ds(base, 16), pl.ds((2 * dr + dc) * MID, MID)] = (
                            cells[dc].astype(BF)
                        )
        return carry

    lax.fori_loop(0, OUT // 16, combine, 0)

    loads[2].wait()

    def res_pair(pair, carry):
        for frame in range(FRAMES):
            left, right, weights = [], [], []
            for tap, src in taps_of(frame):
                for d in range(3):
                    left.append(norm_cols[src * 8 + 2 * pair + d])
                    right.append(norm_cols[src * 8 + 2 * pair + 1 + d])
                weights += [w_res[(tap - 1) * 9 + k] for k in range(9)]
            data = jnp.concatenate(
                [jnp.concatenate(left, axis=0), jnp.concatenate(right, axis=0)], axis=1
            )
            summed = jnp.dot(jnp.concatenate(weights, axis=1), data, preferred_element_type=F32)
            for k in range(2):
                value = first[frame * 8 + 2 * pair + k + 1].astype(F32) + (
                    summed[:, k * COLS : (k + 1) * COLS] + bias_mid[2]
                )
                block[frame * 6 + 2 * pair + k] = value.astype(BF)
        return carry

    lax.fori_loop(0, 3, res_pair, 0)

    loads[3].wait()

    def time_pair(pair, carry):
        for frame in range(FRAMES):
            taps = taps_of(frame)
            data = jnp.concatenate(
                [
                    jnp.concatenate([block[src * 6 + 2 * pair + k] for _, src in taps], axis=0)
                    for k in range(2)
                ],
                axis=1,
            )
            weight = jnp.concatenate([w_time[tap - 1] for tap, _ in taps], axis=1)
            summed = jnp.dot(weight, data, preferred_element_type=F32)
            for k in range(2):
                row_mask = mask_at(frame, row_base - 1 + 2 * pair + k)
                for half in range(2):
                    value = (
                        summed[half * MID : (half + 1) * MID, k * COLS : (k + 1) * COLS]
                        + bias_time[pl.ds(half * MID, MID), :]
                    ) * row_mask
                    at = (2 * frame + half) * 6 + 2 * pair + k
                    for tap, moved in enumerate(shifts(value)):
                        time_cols[at, pl.ds(tap * MID, MID), :] = moved.astype(BF)
        return carry

    lax.fori_loop(0, 3, time_pair, 0)

    def out_copy(frame, slot):
        return pltpu.make_async_copy(out_buf.at[slot], out_hbm.at[:, frame], out_sems.at[slot])

    def up_frame(frame, carry):
        slot = frame % 2

        @pl.when(frame >= 2)
        def _():
            out_copy(frame, slot).wait()

        for pair in range(2):
            for pr in range(2):
                done = []
                for pc in range(2):
                    data = jnp.concatenate(
                        [
                            jnp.concatenate(
                                [
                                    time_cols[
                                        frame * 6 + 2 * pair + k + pr + dr,
                                        pl.ds(pc * MID, 2 * MID),
                                        :,
                                    ]
                                    for dr in range(2)
                                ],
                                axis=0,
                            )
                            for k in range(2)
                        ],
                        axis=1,
                    )
                    done.append(
                        jnp.dot(w_phase[2 * pr + pc], data, preferred_element_type=F32)
                    )
                for k in range(2):
                    row_mask = mask_at(frame // 2, row_base + 2 * pair + k)
                    mixed = jnp.concatenate(
                        [
                            ((d[:, k * COLS : (k + 1) * COLS] + bias_up[...]) * row_mask).astype(BF)
                            for d in done
                        ],
                        axis=1,
                    )
                    wide = jnp.dot(mixed, spread[...], preferred_element_type=F32)
                    at = 2 * (2 * pair + k) + pr
                    for half in range(2):
                        tall[half, pl.ds(at, OUT, stride=8), :] = wide[
                            :, half * COLS : (half + 1) * COLS
                        ]
        for half in range(2):
            out_buf[slot, :, :, pl.ds(half * COLS, COLS)] = (
                tall[half].reshape(OUT, 8, COLS).astype(BF)
            )
        out_copy(frame, slot).start()
        return carry

    lax.fori_loop(0, 2 * FRAMES, up_frame, 0)
    out_copy(2, 0).wait()
    out_copy(3, 1).wait()


def decode(info, rims, vectors, weights):
    hbm = pl.BlockSpec(memory_space=pl.ANY)
    vmem = pl.BlockSpec(memory_space=pltpu.VMEM)
    return pl.pallas_call(
        decode_kernel,
        out_shape=jax.ShapeDtypeStruct((OUT, 2 * FRAMES, 2 * ROWS, 2 * COLS), BF),
        in_specs=[pl.BlockSpec(memory_space=pltpu.SMEM)] + [vmem] * 9 + [hbm] * 4,
        out_specs=hbm,
        scratch_shapes=[
            pltpu.VMEM((27 * LAT, MID), BF),
            pltpu.VMEM((18, MID, MID), BF),
            pltpu.VMEM((2, 2 * MID, MID), BF),
            pltpu.VMEM((9, OUT, MID), BF),
            pltpu.VMEM((FRAMES, 10, 3 * LAT, COLS), BF),
            pltpu.VMEM((FRAMES * 8, MID, COLS), F32),
            pltpu.VMEM((FRAMES * 8, MID, COLS), BF),
            pltpu.VMEM((FRAMES * 8, 3 * MID, COLS), BF),
            pltpu.VMEM((FRAMES * 6, MID, COLS), BF),
            pltpu.VMEM((2 * FRAMES * 6, 3 * MID, COLS), BF),
            pltpu.VMEM((4, OUT, 4 * MID), BF),
            pltpu.VMEM((3, MID, COLS), F32),
            pltpu.VMEM((2 * MID, COLS), F32),
            pltpu.VMEM((OUT, COLS), F32),
            pltpu.VMEM((2 * COLS, 2 * COLS), BF),
            pltpu.VMEM((2, OUT * 8, COLS), F32),
            pltpu.VMEM((2, OUT, 8, 2 * COLS), BF),
            pltpu.SemaphoreType.DMA((4,)),
            pltpu.SemaphoreType.DMA((2,)),
        ],
        compiler_params=pltpu.CompilerParams(vmem_limit_bytes=44 << 20),
        cost_estimate=pl.CostEstimate(
            flops=13_000_000_000, bytes_accessed=13_000_000, transcendentals=800_000
        ),
    )(info, *rims, *vectors, *weights)


def pick(options, chosen):
    result = options[0]
    for k in range(1, len(options)):
        result = jnp.where(chosen == k, options[k], result)
    return result


def on_device(
    latents,
    piece_dest,
    frames,
    heights,
    widths,
    w_in,
    b_in,
    gain_norm,
    w_res,
    b_res,
    w_time,
    b_time,
    w_up,
    b_up,
):
    group, tile = lax.axis_index("req"), lax.axis_index("tile")
    ring = 4
    along_x, along_z = group // ring, group % ring

    def shift_x(value, k):
        return lax.ppermute(
            value,
            "req",
            [(x * ring + z, (x + k) % ring * ring + z) for x in range(ring) for z in range(ring)],
        )

    def shift_z(value, k):
        return lax.ppermute(
            value,
            "req",
            [(x * ring + z, x * ring + (z + k) % ring) for x in range(ring) for z in range(ring)],
        )

    wanted = piece_dest.reshape(ring * ring, -1)[:, 0] // (FRAMES * 32)
    held = [latents] + [shift_x(latents, k) for k in range(1, ring)]
    held_for = [wanted[(along_x - k) % ring * ring + along_z] for k in range(ring)]

    def select_for(target):
        chosen = jnp.int32(0)
        for k in range(1, ring):
            chosen = jnp.where(held_for[k] == target, k, chosen)
        return pick(held, chosen)

    arrived = [select_for(group)]
    for k in range(1, ring):
        arrived.append(shift_z(select_for(along_x * ring + (along_z + k) % ring), k))
    source = jnp.argmax(wanted == group).astype(jnp.int32)
    mine = pick(arrived, (along_z - source % ring) % ring)

    late = tile >= 4
    upper, lower = mine[0:7], mine[1:8]
    head, tail = mine[0:3], mine[5:8]
    quarter = range(4)
    rims = [
        lax.ppermute(
            jnp.where(late, lower, upper),
            "tile",
            [(s, 2 * s) for s in quarter] + [(4 + s, 2 * s + 1) for s in quarter],
        ),
        lax.ppermute(
            jnp.where(late, upper, lower),
            "tile",
            [(s, 2 * s + 1) for s in quarter] + [(4 + s, 2 * s) for s in quarter],
        ),
        lax.ppermute(
            jnp.where(late, tail, head),
            "tile",
            [(s, 2 * s - 1) for s in quarter if s > 0]
            + [(4 + s, 2 * s + 2) for s in quarter if s < 3],
        ),
        lax.ppermute(
            jnp.where(late, head, tail),
            "tile",
            [(s, 2 * s + 2) for s in quarter if s < 3]
            + [(4 + s, 2 * s - 1) for s in quarter if s > 0],
        ),
    ]
    info = jnp.stack(
        [tile % 2, frames[group], heights[group], widths[group], tile * ROWS]
    ).astype(jnp.int32)
    vectors = [v.reshape(1, -1) for v in (b_in, gain_norm, b_res, b_time, b_up)]
    weights = [
        jnp.swapaxes(w_in, 3, 4).reshape(27 * LAT, MID),
        w_res.reshape(27, MID, MID),
        w_time,
        w_up.reshape(9, OUT, MID),
    ]
    return decode(info, rims, vectors, weights)[None]


def solution(mesh):
    return jax.shard_map(
        on_device,
        mesh=mesh,
        in_specs=(P(("req", "tile"), None, None),) + (P(),) * 13,
        out_specs=P("req", None, None, "tile", None),
        check_vma=False,
    )
```

```python
import functools

import jax
import jax.numpy as jnp
from jax import lax
from jax.experimental import pallas as pl
from jax.experimental.pallas import tpu as pltpu
from jax.sharding import PartitionSpec as P

LAT = 16
MID = 384
OUT = 192
FRAMES = 2
ROWS = 4
COLS = 128
BF = jnp.bfloat16
F32 = jnp.float32


def taps_of(frame):
    return [(tap, frame - 2 + tap) for tap in range(3) if frame - 2 + tap >= 0]


def column(vec_ref):
    return jnp.transpose(jnp.broadcast_to(vec_ref[...][None, :], (COLS, vec_ref.shape[0])))


def shifts(x):
    col = lax.broadcasted_iota(jnp.int32, x.shape, 1)
    before = jnp.where(col == 0, 0.0, pltpu.roll(x, 1, 1))
    after = jnp.where(col == COLS - 1, 0.0, pltpu.roll(x, COLS - 1, 1))
    return before, x, after


RING = 4
PICK_Z, PICK_MINE, LATE, ODD, REGION, N_MASK = 0, 16, 20, 21, 22, 48


def mask_kernel(piece_dest, frames, heights, widths, masks):
    group, tile = lax.axis_index("req"), lax.axis_index("tile")
    along_x, along_z = lax.div(group, RING), lax.rem(group, RING)
    per_group = piece_dest.shape[0] // (RING * RING)

    def wanted(p):
        return lax.div(piece_dest[p * per_group], per_group)

    def put(row, flag):
        value = jnp.where(flag, 1.0, 0.0).astype(F32)
        masks[pl.ds(row, 1), :] = jnp.full((1, COLS), value, F32)

    held_for = [wanted(lax.rem(along_x - k + RING, RING) * RING + along_z) for k in range(RING)]
    for j in range(RING):
        target = along_x * RING + lax.rem(along_z + j, RING)
        for k in range(RING):
            put(PICK_Z + RING * j + k, held_for[k] == target)
    source_z = jnp.int32(0)
    for p in range(RING * RING):
        source_z = jnp.where(wanted(p) == group, p % RING, source_z)
    offset = lax.rem(along_z - source_z + RING, RING)
    for j in range(RING):
        put(PICK_MINE + j, offset == j)
    put(LATE, tile >= 4)
    put(ODD, lax.rem(tile, 2) == 1)
    cols = lax.broadcasted_iota(jnp.int32, (1, COLS), 1)
    inside_cols = (cols < widths[group]).astype(F32)
    for frame in range(FRAMES):
        for row in range(10):
            at = tile * ROWS - 3 + row
            inside = (frame < frames[group]) & (at >= 0) & (at < heights[group])
            value = inside_cols * jnp.where(inside, 1.0, 0.0).astype(F32)
            masks[pl.ds(REGION + 10 * frame + row, 1), :] = value
    masks[pl.ds(REGION + 20, N_MASK - REGION - 20), :] = jnp.zeros((N_MASK - REGION - 20, COLS), F32)


def make_masks(piece_dest, frames, heights, widths):
    return pl.pallas_call(
        mask_kernel,
        out_shape=jax.ShapeDtypeStruct((N_MASK, COLS), F32),
        in_specs=[pl.BlockSpec(memory_space=pltpu.SMEM)] * 4,
        out_specs=pl.BlockSpec(memory_space=pltpu.VMEM),
        cost_estimate=pl.CostEstimate(flops=100_000, bytes_accessed=30_000, transcendentals=0),
    )(piece_dest, frames, heights, widths)


def prepare_kernel(b_in, gain, b_res, b_time, b_up, w_up, w_phase, bias):
    for at, vec in enumerate((b_in, gain, b_res)):
        bias[pl.ds(at * MID, MID), :] = column(vec)
    bias[pl.ds(3 * MID, 2 * MID), :] = column(b_time)
    bias[pl.ds(5 * MID, OUT), :] = column(b_up)

    def two(phase, taps):
        return (taps[0], taps[1] + taps[2]) if phase == 0 else (taps[0] + taps[1], taps[2])

    def combine(at, carry):
        base = pl.multiple_of(at * 16, 16)
        whole = [
            [w_up[3 * d + e, pl.ds(base, 16), :].astype(F32) for e in range(3)] for d in range(3)
        ]
        for pr in range(2):
            rows = [two(pr, [whole[d][e] for d in range(3)]) for e in range(3)]
            for dr in range(2):
                for pc in range(2):
                    cells = two(pc, [rows[e][dr] for e in range(3)])
                    for dc in range(2):
                        w_phase[2 * pr + pc, pl.ds(base, 16), pl.ds((2 * dr + dc) * MID, MID)] = (
                            cells[dc].astype(BF)
                        )
        return carry

    lax.fori_loop(0, OUT // 16, combine, 0)


def prepare(vectors, w_up):
    vmem = pl.BlockSpec(memory_space=pltpu.VMEM)
    return pl.pallas_call(
        prepare_kernel,
        out_shape=(
            jax.ShapeDtypeStruct((4, OUT, 4 * MID), BF),
            jax.ShapeDtypeStruct((5 * MID + OUT, COLS), F32),
        ),
        in_specs=[vmem] * 6,
        out_specs=(vmem, vmem),
        cost_estimate=pl.CostEstimate(
            flops=10_000_000, bytes_accessed=5_000_000, transcendentals=0
        ),
    )(*vectors, w_up)


def decode_kernel(
    masks,
    rim_a,
    rim_b,
    rim_c,
    rim_d,
    bias_hbm,
    w_in_hbm,
    w_res_hbm,
    w_time_hbm,
    w_phase_hbm,
    out_hbm,
    w_in,
    w_res,
    w_time,
    w_phase,
    bias,
    lat_cols,
    conv,
    first,
    norm_cols,
    block,
    time_cols,
    spread,
    tall,
    out_buf,
    in_sems,
    out_sems,
):
    loads = [
        pltpu.make_async_copy(w_in_hbm, w_in, in_sems.at[0]),
        pltpu.make_async_copy(bias_hbm, bias, in_sems.at[1]),
        pltpu.make_async_copy(w_res_hbm.at[pl.ds(9, 18)], w_res, in_sems.at[2]),
        pltpu.make_async_copy(w_time_hbm.at[pl.ds(1, 2)], w_time, in_sems.at[3]),
        pltpu.make_async_copy(w_phase_hbm, w_phase, in_sems.at[4]),
    ]
    for load in loads:
        load.start()

    def bias_of(at, count):
        return bias[pl.ds(at, count), :]

    def mask_at(frame, row):
        return masks[pl.ds(REGION + 10 * frame + row, 1), :]

    key = lax.broadcasted_iota(jnp.int32, (2 * COLS, 2 * COLS), 0)
    place = lax.broadcasted_iota(jnp.int32, (2 * COLS, 2 * COLS), 1)
    spread[...] = (key == (place % 2) * COLS + place // 2).astype(F32).astype(BF)
    odd = jnp.broadcast_to(masks[pl.ds(ODD, 1), :], (LAT, COLS)) > 0.5

    for frame in range(FRAMES):
        main_even, main_odd = (rim_a, rim_b) if frame == 0 else (rim_b, rim_a)
        rest_even, rest_odd = (rim_d, rim_c) if frame == 0 else (rim_c, rim_d)
        for row in range(10):
            even = rest_even[row] if row < 3 else main_even[row - 3]
            other = main_odd[row] if row < 7 else rest_odd[row - 7]
            value = jnp.where(odd, other.astype(F32), even.astype(F32))
            value = value * mask_at(frame, row)
            for at, moved in enumerate(shifts(value)):
                lat_cols[frame, row, pl.ds(at * LAT, LAT), :] = moved.astype(BF)

    loads[0].wait()
    for frame in range(FRAMES):
        taps = taps_of(frame)
        weight = w_in[pl.ds(taps[0][0] * 9 * LAT, len(taps) * 9 * LAT), :]
        pieces = []
        for row in range(8):
            pieces.append(
                jnp.concatenate(
                    [lat_cols[src, row + d] for _, src in taps for d in range(3)], axis=0
                )
            )
        data = jnp.concatenate(pieces, axis=1)
        summed = lax.dot_general(
            weight, data, (((0,), (0,)), ((), ())), preferred_element_type=F32
        )
        for row in range(8):
            conv[frame * 8 + row] = summed[:, row * COLS : (row + 1) * COLS]

    loads[1].wait()

    def norm_row(at, carry):
        frame, row = at // 8, at % 8
        value = (conv[at] + bias_of(0, MID)).astype(BF)
        first[at] = value
        value = value.astype(F32)
        mean = jnp.sum(value * value, axis=0, keepdims=True) * (1.0 / MID)
        scaled = value * lax.rsqrt(mean + 1e-6) * bias_of(MID, MID)
        normed = scaled / (1.0 + jnp.exp(-scaled)) * mask_at(frame, row + 1)
        for tap, moved in enumerate(shifts(normed)):
            norm_cols[at, pl.ds(tap * MID, MID), :] = moved.astype(BF)
        return carry

    lax.fori_loop(0, FRAMES * 8, norm_row, 0)

    loads[2].wait()

    def res_pair(pair, carry):
        for frame in range(FRAMES):
            left, right, weights = [], [], []
            for tap, src in taps_of(frame):
                for d in range(3):
                    left.append(norm_cols[src * 8 + 2 * pair + d])
                    right.append(norm_cols[src * 8 + 2 * pair + 1 + d])
                weights += [w_res[(tap - 1) * 9 + k] for k in range(9)]
            data = jnp.concatenate(
                [jnp.concatenate(left, axis=0), jnp.concatenate(right, axis=0)], axis=1
            )
            summed = jnp.dot(jnp.concatenate(weights, axis=1), data, preferred_element_type=F32)
            for k in range(2):
                value = first[frame * 8 + 2 * pair + k + 1].astype(F32) + (
                    summed[:, k * COLS : (k + 1) * COLS] + bias_of(2 * MID, MID)
                )
                block[frame * 6 + 2 * pair + k] = value.astype(BF)
        return carry

    lax.fori_loop(0, 3, res_pair, 0)

    loads[3].wait()

    def time_pair(pair, carry):
        for frame in range(FRAMES):
            taps = taps_of(frame)
            data = jnp.concatenate(
                [
                    jnp.concatenate([block[src * 6 + 2 * pair + k] for _, src in taps], axis=0)
                    for k in range(2)
                ],
                axis=1,
            )
            weight = jnp.concatenate([w_time[tap - 1] for tap, _ in taps], axis=1)
            summed = jnp.dot(weight, data, preferred_element_type=F32)
            for k in range(2):
                row_mask = mask_at(frame, 2 * pair + k + 2)
                for half in range(2):
                    value = (
                        summed[half * MID : (half + 1) * MID, k * COLS : (k + 1) * COLS]
                        + bias_of((3 + half) * MID, MID)
                    ) * row_mask
                    at = (2 * frame + half) * 6 + 2 * pair + k
                    for tap, moved in enumerate(shifts(value)):
                        time_cols[at, pl.ds(tap * MID, MID), :] = moved.astype(BF)
        return carry

    lax.fori_loop(0, 3, time_pair, 0)

    def out_copy(frame, slot):
        return pltpu.make_async_copy(out_buf.at[slot], out_hbm.at[:, frame], out_sems.at[slot])

    def up_frame(frame, carry):
        slot = frame % 2

        @pl.when(frame >= 2)
        def _():
            out_copy(frame, slot).wait()

        for pair in range(2):
            for pr in range(2):
                done = []
                for pc in range(2):
                    data = jnp.concatenate(
                        [
                            jnp.concatenate(
                                [
                                    time_cols[
                                        frame * 6 + 2 * pair + k + pr + dr,
                                        pl.ds(pc * MID, 2 * MID),
                                        :,
                                    ]
                                    for dr in range(2)
                                ],
                                axis=0,
                            )
                            for k in range(2)
                        ],
                        axis=1,
                    )
                    done.append(
                        jnp.dot(w_phase[2 * pr + pc], data, preferred_element_type=F32)
                    )
                for k in range(2):
                    row_mask = mask_at(frame // 2, 2 * pair + k + 3)
                    mixed = jnp.concatenate(
                        [
                            ((d[:, k * COLS : (k + 1) * COLS] + bias_of(5 * MID, OUT)) * row_mask).astype(BF)
                            for d in done
                        ],
                        axis=1,
                    )
                    wide = jnp.dot(mixed, spread[...], preferred_element_type=F32)
                    at = 2 * (2 * pair + k) + pr
                    for half in range(2):
                        tall[half, pl.ds(at, OUT, stride=8), :] = wide[
                            :, half * COLS : (half + 1) * COLS
                        ]
        for half in range(2):
            out_buf[slot, :, :, pl.ds(half * COLS, COLS)] = (
                tall[half].reshape(OUT, 8, COLS).astype(BF)
            )
        out_copy(frame, slot).start()
        return carry

    loads[4].wait()
    lax.fori_loop(0, 2 * FRAMES, up_frame, 0)
    out_copy(2, 0).wait()
    out_copy(3, 1).wait()


def decode(masks, rims, weights):
    hbm = pl.BlockSpec(memory_space=pltpu.HBM)
    anywhere = pl.BlockSpec(memory_space=pl.ANY)
    vmem = pl.BlockSpec(memory_space=pltpu.VMEM)
    return pl.pallas_call(
        decode_kernel,
        out_shape=jax.ShapeDtypeStruct((OUT, 2 * FRAMES, 2 * ROWS, 2 * COLS), BF),
        in_specs=[vmem] * 5 + [anywhere] + [hbm] * 3 + [anywhere],
        out_specs=hbm,
        scratch_shapes=[
            pltpu.VMEM((27 * LAT, MID), BF),
            pltpu.VMEM((18, MID, MID), BF),
            pltpu.VMEM((2, 2 * MID, MID), BF),
            pltpu.VMEM((4, OUT, 4 * MID), BF),
            pltpu.VMEM((5 * MID + OUT, COLS), F32),
            pltpu.VMEM((FRAMES, 10, 3 * LAT, COLS), BF),
            pltpu.VMEM((FRAMES * 8, MID, COLS), F32),
            pltpu.VMEM((FRAMES * 8, MID, COLS), BF),
            pltpu.VMEM((FRAMES * 8, 3 * MID, COLS), BF),
            pltpu.VMEM((FRAMES * 6, MID, COLS), BF),
            pltpu.VMEM((2 * FRAMES * 6, 3 * MID, COLS), BF),
            pltpu.VMEM((2 * COLS, 2 * COLS), BF),
            pltpu.VMEM((2, OUT * 8, COLS), F32),
            pltpu.VMEM((2, OUT, 8, 2 * COLS), BF),
            pltpu.SemaphoreType.DMA((5,)),
            pltpu.SemaphoreType.DMA((2,)),
        ],
        compiler_params=pltpu.CompilerParams(vmem_limit_bytes=61 << 20),
        cost_estimate=pl.CostEstimate(
            flops=13_000_000_000, bytes_accessed=13_000_000, transcendentals=800_000
        ),
    )(masks, *rims, *weights)


def pick(options, masks, base):
    result = options[0]
    for k in range(1, len(options)):
        result = jnp.where(masks[base + k] > 0.5, options[k], result)
    return result


def on_device(
    latents,
    piece_dest,
    frames,
    heights,
    widths,
    w_in,
    b_in,
    gain_norm,
    w_res,
    b_res,
    w_time,
    b_time,
    w_up,
    b_up,
):
    ring = RING
    masks = make_masks(piece_dest, frames, heights, widths)
    w_up = w_up.reshape(9, OUT, MID)
    w_phase, bias = prepare((b_in, gain_norm, b_res, b_time, b_up), w_up)

    def shift_x(value, k):
        return lax.ppermute(
            value,
            "req",
            [(x * ring + z, (x + k) % ring * ring + z) for x in range(ring) for z in range(ring)],
        )

    def shift_z(value, k):
        return lax.ppermute(
            value,
            "req",
            [(x * ring + z, x * ring + (z + k) % ring) for x in range(ring) for z in range(ring)],
        )

    held = [latents] + [shift_x(latents, k) for k in range(1, ring)]
    picked = [pick(held, masks, PICK_Z + ring * k) for k in range(ring)]
    arrived = [picked[0]] + [shift_z(picked[k], k) for k in range(1, ring)]
    mine = pick(arrived, masks, PICK_MINE)

    late = masks[LATE] > 0.5
    upper, lower = mine[0:7], mine[1:8]
    head, tail = mine[0:3], mine[5:8]
    quarter = range(4)
    rims = [
        lax.ppermute(
            jnp.where(late, lower, upper),
            "tile",
            [(s, 2 * s) for s in quarter] + [(4 + s, 2 * s + 1) for s in quarter],
        ),
        lax.ppermute(
            jnp.where(late, upper, lower),
            "tile",
            [(s, 2 * s + 1) for s in quarter] + [(4 + s, 2 * s) for s in quarter],
        ),
        lax.ppermute(
            jnp.where(late, tail, head),
            "tile",
            [(s, 2 * s - 1) for s in quarter if s > 0]
            + [(4 + s, 2 * s + 2) for s in quarter if s < 3],
        ),
        lax.ppermute(
            jnp.where(late, head, tail),
            "tile",
            [(s, 2 * s + 2) for s in quarter if s < 3]
            + [(4 + s, 2 * s - 1) for s in quarter if s > 0],
        ),
    ]
    weights = [
        bias,
        jnp.swapaxes(w_in, 3, 4).reshape(27 * LAT, MID),
        w_res.reshape(27, MID, MID),
        w_time,
        w_phase,
    ]
    return decode(masks, rims, weights)[None]


def solution(mesh):
    return jax.shard_map(
        on_device,
        mesh=mesh,
        in_specs=(P(("req", "tile"), None, None),) + (P(),) * 13,
        out_specs=P("req", None, None, "tile", None),
        check_vma=False,
    )
```

```python
import functools

import jax
import jax.numpy as jnp
from jax import lax
from jax.experimental import pallas as pl
from jax.experimental.pallas import tpu as pltpu
from jax.sharding import PartitionSpec as P

LAT = 16
MID = 384
OUT = 192
FRAMES = 2
ROWS = 4
COLS = 128
BF = jnp.bfloat16
F32 = jnp.float32


def taps_of(frame):
    return [(tap, frame - 2 + tap) for tap in range(3) if frame - 2 + tap >= 0]


def column(vec_ref):
    return jnp.transpose(jnp.broadcast_to(vec_ref[...][None, :], (COLS, vec_ref.shape[0])))


def shifts(x):
    col = lax.broadcasted_iota(jnp.int32, x.shape, 1)
    zero = jnp.zeros_like(x)
    before = jnp.where(col == 0, zero, pltpu.roll(x, 1, 1))
    after = jnp.where(col == COLS - 1, zero, pltpu.roll(x, COLS - 1, 1))
    return before, x, after


RING = 4
PICK_Z, PICK_MINE, LATE, ODD, REGION, N_MASK = 0, 16, 20, 21, 22, 48


def mask_kernel(piece_dest, frames, heights, widths, masks):
    group, tile = lax.axis_index("req"), lax.axis_index("tile")
    along_x, along_z = lax.div(group, RING), lax.rem(group, RING)
    per_group = piece_dest.shape[0] // (RING * RING)

    def wanted(p):
        return lax.div(piece_dest[p * per_group], per_group)

    def put(row, flag):
        value = jnp.where(flag, 1.0, 0.0).astype(F32)
        masks[pl.ds(row, 1), :] = jnp.full((1, COLS), value, F32)

    held_for = [wanted(lax.rem(along_x - k + RING, RING) * RING + along_z) for k in range(RING)]
    for j in range(RING):
        target = along_x * RING + lax.rem(along_z + j, RING)
        for k in range(RING):
            put(PICK_Z + RING * j + k, held_for[k] == target)
    source_z = jnp.int32(0)
    for p in range(RING * RING):
        source_z = jnp.where(wanted(p) == group, p % RING, source_z)
    offset = lax.rem(along_z - source_z + RING, RING)
    for j in range(RING):
        put(PICK_MINE + j, offset == j)
    put(LATE, tile >= 4)
    put(ODD, lax.rem(tile, 2) == 1)
    cols = lax.broadcasted_iota(jnp.int32, (1, COLS), 1)
    inside_cols = (cols < widths[group]).astype(F32)
    for frame in range(FRAMES):
        for row in range(10):
            at = tile * ROWS - 3 + row
            inside = (frame < frames[group]) & (at >= 0) & (at < heights[group])
            value = inside_cols * jnp.where(inside, 1.0, 0.0).astype(F32)
            masks[pl.ds(REGION + 10 * frame + row, 1), :] = value
    masks[pl.ds(REGION + 20, N_MASK - REGION - 20), :] = jnp.zeros((N_MASK - REGION - 20, COLS), F32)


def make_masks(piece_dest, frames, heights, widths):
    return pl.pallas_call(
        mask_kernel,
        out_shape=jax.ShapeDtypeStruct((N_MASK, COLS), F32),
        in_specs=[pl.BlockSpec(memory_space=pltpu.SMEM)] * 4,
        out_specs=pl.BlockSpec(memory_space=pltpu.VMEM),
        cost_estimate=pl.CostEstimate(flops=100_000, bytes_accessed=30_000, transcendentals=0),
    )(piece_dest, frames, heights, widths)


def prepare_kernel(b_in, gain, b_res, b_time, b_up, w_up, w_phase, bias):
    for at, vec in enumerate((b_in, gain, b_res)):
        bias[pl.ds(at * MID, MID), :] = column(vec)
    bias[pl.ds(3 * MID, 2 * MID), :] = column(b_time)
    bias[pl.ds(5 * MID, OUT), :] = column(b_up)

    def two(phase, taps):
        return (taps[0], taps[1] + taps[2]) if phase == 0 else (taps[0] + taps[1], taps[2])

    def combine(at, carry):
        base = pl.multiple_of(at * 16, 16)
        whole = [
            [w_up[3 * d + e, pl.ds(base, 16), :].astype(F32) for e in range(3)] for d in range(3)
        ]
        for pr in range(2):
            rows = [two(pr, [whole[d][e] for d in range(3)]) for e in range(3)]
            for dr in range(2):
                for pc in range(2):
                    cells = two(pc, [rows[e][dr] for e in range(3)])
                    for dc in range(2):
                        w_phase[2 * pr + pc, pl.ds(base, 16), pl.ds((2 * dr + dc) * MID, MID)] = (
                            cells[dc].astype(BF)
                        )
        return carry

    lax.fori_loop(0, OUT // 16, combine, 0)


def prepare(vectors, w_up):
    vmem = pl.BlockSpec(memory_space=pltpu.VMEM)
    return pl.pallas_call(
        prepare_kernel,
        out_shape=(
            jax.ShapeDtypeStruct((4, OUT, 4 * MID), BF),
            jax.ShapeDtypeStruct((5 * MID + OUT, COLS), F32),
        ),
        in_specs=[vmem] * 6,
        out_specs=(vmem, vmem),
        cost_estimate=pl.CostEstimate(
            flops=10_000_000, bytes_accessed=5_000_000, transcendentals=0
        ),
    )(*vectors, w_up)


def decode_kernel(
    masks,
    rim_a,
    rim_b,
    rim_c,
    rim_d,
    bias_hbm,
    w_in_hbm,
    w_res_hbm,
    w_time_hbm,
    w_phase_hbm,
    out_hbm,
    w_in,
    w_res,
    w_time,
    w_phase,
    bias,
    lat_cols,
    conv,
    first,
    norm_cols,
    block,
    time_cols,
    spread,
    tall,
    out_buf,
    in_sems,
    out_sems,
):
    loads = [
        pltpu.make_async_copy(w_in_hbm, w_in, in_sems.at[0]),
        pltpu.make_async_copy(bias_hbm, bias, in_sems.at[1]),
        pltpu.make_async_copy(w_res_hbm.at[pl.ds(9, 18)], w_res, in_sems.at[2]),
        pltpu.make_async_copy(w_time_hbm.at[pl.ds(1, 2)], w_time, in_sems.at[3]),
        pltpu.make_async_copy(w_phase_hbm, w_phase, in_sems.at[4]),
    ]
    for load in loads:
        load.start()

    def bias_of(at, count):
        return bias[pl.ds(at, count), :]

    def mask_at(frame, row):
        return masks[pl.ds(REGION + 10 * frame + row, 1), :]

    key = lax.broadcasted_iota(jnp.int32, (2 * COLS, 2 * COLS), 0)
    place = lax.broadcasted_iota(jnp.int32, (2 * COLS, 2 * COLS), 1)
    spread[...] = (key == (place % 2) * COLS + place // 2).astype(F32).astype(BF)
    odd = jnp.broadcast_to(masks[pl.ds(ODD, 1), :], (LAT, COLS)) > 0.5

    for frame in range(FRAMES):
        main_even, main_odd = (rim_a, rim_b) if frame == 0 else (rim_b, rim_a)
        rest_even, rest_odd = (rim_d, rim_c) if frame == 0 else (rim_c, rim_d)
        for row in range(10):
            even = rest_even[row] if row < 3 else main_even[row - 3]
            other = main_odd[row] if row < 7 else rest_odd[row - 7]
            value = jnp.where(odd, other.astype(F32), even.astype(F32))
            value = value * mask_at(frame, row)
            for at, moved in enumerate(shifts(value.astype(BF))):
                lat_cols[frame, row, pl.ds(at * LAT, LAT), :] = moved

    loads[0].wait()
    for frame in range(FRAMES):
        taps = taps_of(frame)
        weight = w_in[pl.ds(taps[0][0] * 9 * LAT, len(taps) * 9 * LAT), :]
        pieces = []
        for row in range(8):
            pieces.append(
                jnp.concatenate(
                    [lat_cols[src, row + d] for _, src in taps for d in range(3)], axis=0
                )
            )
        data = jnp.concatenate(pieces, axis=1)
        summed = lax.dot_general(
            weight, data, (((0,), (0,)), ((), ())), preferred_element_type=F32
        )
        for row in range(8):
            conv[frame * 8 + row] = summed[:, row * COLS : (row + 1) * COLS]

    loads[1].wait()

    def norm_row(at, carry):
        frame, row = at // 8, at % 8
        value = (conv[at] + bias_of(0, MID)).astype(BF)
        first[at] = value
        value = value.astype(F32)
        mean = jnp.sum(value * value, axis=0, keepdims=True) * (1.0 / MID)
        scaled = value * lax.rsqrt(mean + 1e-6) * bias_of(MID, MID)
        half = 0.5 * scaled
        normed = (half + half * jnp.tanh(half)) * mask_at(frame, row + 1)
        for tap, moved in enumerate(shifts(normed.astype(BF))):
            norm_cols[at, pl.ds(tap * MID, MID), :] = moved
        return carry

    lax.fori_loop(0, FRAMES * 8, norm_row, 0, unroll=2)

    loads[2].wait()

    def res_pair(pair, carry):
        for frame in range(FRAMES):
            left, right, weights = [], [], []
            for tap, src in taps_of(frame):
                for d in range(3):
                    left.append(norm_cols[src * 8 + 2 * pair + d])
                    right.append(norm_cols[src * 8 + 2 * pair + 1 + d])
                weights += [w_res[(tap - 1) * 9 + k] for k in range(9)]
            data = jnp.concatenate(
                [jnp.concatenate(left, axis=0), jnp.concatenate(right, axis=0)], axis=1
            )
            summed = jnp.dot(jnp.concatenate(weights, axis=1), data, preferred_element_type=F32)
            for k in range(2):
                value = first[frame * 8 + 2 * pair + k + 1].astype(F32) + (
                    summed[:, k * COLS : (k + 1) * COLS] + bias_of(2 * MID, MID)
                )
                block[frame * 6 + 2 * pair + k] = value.astype(BF)
        return carry

    lax.fori_loop(0, 3, res_pair, 0)

    loads[3].wait()

    def time_pair(pair, carry):
        for frame in range(FRAMES):
            taps = taps_of(frame)
            data = jnp.concatenate(
                [
                    jnp.concatenate([block[src * 6 + 2 * pair + k] for _, src in taps], axis=0)
                    for k in range(2)
                ],
                axis=1,
            )
            weight = jnp.concatenate([w_time[tap - 1] for tap, _ in taps], axis=1)
            summed = jnp.dot(weight, data, preferred_element_type=F32)
            for k in range(2):
                row_mask = mask_at(frame, 2 * pair + k + 2)
                for half in range(2):
                    value = (
                        summed[half * MID : (half + 1) * MID, k * COLS : (k + 1) * COLS]
                        + bias_of((3 + half) * MID, MID)
                    ) * row_mask
                    at = (2 * frame + half) * 6 + 2 * pair + k
                    for tap, moved in enumerate(shifts(value.astype(BF))):
                        time_cols[at, pl.ds(tap * MID, MID), :] = moved
        return carry

    lax.fori_loop(0, 3, time_pair, 0)

    def out_copy(frame, slot):
        return pltpu.make_async_copy(out_buf.at[slot], out_hbm.at[:, frame], out_sems.at[slot])

    def up_frame(frame, carry):
        slot = frame % 2

        @pl.when(frame >= 2)
        def _():
            out_copy(frame, slot).wait()

        for pair in range(2):
            for pr in range(2):
                done = []
                for pc in range(2):
                    data = jnp.concatenate(
                        [
                            jnp.concatenate(
                                [
                                    time_cols[
                                        frame * 6 + 2 * pair + k + pr + dr,
                                        pl.ds(pc * MID, 2 * MID),
                                        :,
                                    ]
                                    for dr in range(2)
                                ],
                                axis=0,
                            )
                            for k in range(2)
                        ],
                        axis=1,
                    )
                    done.append(
                        jnp.dot(w_phase[2 * pr + pc], data, preferred_element_type=F32)
                    )
                for k in range(2):
                    row_mask = mask_at(frame // 2, 2 * pair + k + 3)
                    mixed = jnp.concatenate(
                        [
                            ((d[:, k * COLS : (k + 1) * COLS] + bias_of(5 * MID, OUT)) * row_mask).astype(BF)
                            for d in done
                        ],
                        axis=1,
                    )
                    wide = jnp.dot(mixed, spread[...], preferred_element_type=F32)
                    at = 2 * (2 * pair + k) + pr
                    for half in range(2):
                        tall[half, pl.ds(at, OUT, stride=8), :] = wide[
                            :, half * COLS : (half + 1) * COLS
                        ]
        for half in range(2):
            out_buf[slot, :, :, pl.ds(half * COLS, COLS)] = (
                tall[half].reshape(OUT, 8, COLS).astype(BF)
            )
        out_copy(frame, slot).start()
        return carry

    loads[4].wait()
    lax.fori_loop(0, 2 * FRAMES, up_frame, 0)
    out_copy(2, 0).wait()
    out_copy(3, 1).wait()


def decode(masks, rims, weights):
    hbm = pl.BlockSpec(memory_space=pltpu.HBM)
    anywhere = pl.BlockSpec(memory_space=pl.ANY)
    vmem = pl.BlockSpec(memory_space=pltpu.VMEM)
    return pl.pallas_call(
        decode_kernel,
        out_shape=jax.ShapeDtypeStruct((OUT, 2 * FRAMES, 2 * ROWS, 2 * COLS), BF),
        in_specs=[vmem] * 5 + [anywhere] + [hbm] * 3 + [anywhere],
        out_specs=hbm,
        scratch_shapes=[
            pltpu.VMEM((27 * LAT, MID), BF),
            pltpu.VMEM((18, MID, MID), BF),
            pltpu.VMEM((2, 2 * MID, MID), BF),
            pltpu.VMEM((4, OUT, 4 * MID), BF),
            pltpu.VMEM((5 * MID + OUT, COLS), F32),
            pltpu.VMEM((FRAMES, 10, 3 * LAT, COLS), BF),
            pltpu.VMEM((FRAMES * 8, MID, COLS), F32),
            pltpu.VMEM((FRAMES * 8, MID, COLS), BF),
            pltpu.VMEM((FRAMES * 8, 3 * MID, COLS), BF),
            pltpu.VMEM((FRAMES * 6, MID, COLS), BF),
            pltpu.VMEM((2 * FRAMES * 6, 3 * MID, COLS), BF),
            pltpu.VMEM((2 * COLS, 2 * COLS), BF),
            pltpu.VMEM((2, OUT * 8, COLS), F32),
            pltpu.VMEM((2, OUT, 8, 2 * COLS), BF),
            pltpu.SemaphoreType.DMA((5,)),
            pltpu.SemaphoreType.DMA((2,)),
        ],
        compiler_params=pltpu.CompilerParams(vmem_limit_bytes=61 << 20),
        cost_estimate=pl.CostEstimate(
            flops=13_000_000_000, bytes_accessed=13_000_000, transcendentals=800_000
        ),
    )(masks, *rims, *weights)


def pick(options, masks, base):
    result = options[0]
    for k in range(1, len(options)):
        result = jnp.where(masks[base + k] > 0.5, options[k], result)
    return result


def on_device(
    latents,
    piece_dest,
    frames,
    heights,
    widths,
    w_in,
    b_in,
    gain_norm,
    w_res,
    b_res,
    w_time,
    b_time,
    w_up,
    b_up,
):
    ring = RING
    masks = make_masks(piece_dest, frames, heights, widths)
    w_up = w_up.reshape(9, OUT, MID)

    def shift_x(value, k):
        return lax.ppermute(
            value,
            "req",
            [(x * ring + z, (x + k) % ring * ring + z) for x in range(ring) for z in range(ring)],
        )

    def shift_z(value, k):
        return lax.ppermute(
            value,
            "req",
            [(x * ring + z, x * ring + (z + k) % ring) for x in range(ring) for z in range(ring)],
        )

    held = [latents] + [shift_x(latents, k) for k in range(1, ring)]
    picked = [pick(held, masks, PICK_Z + ring * k) for k in range(ring)]
    first_pick, w_up = lax.optimization_barrier((picked[0], w_up))
    picked[0] = first_pick
    w_phase, bias = prepare((b_in, gain_norm, b_res, b_time, b_up), w_up)
    arrived = [picked[0]] + [shift_z(picked[k], k) for k in range(1, ring)]
    masks, w_phase, bias = lax.optimization_barrier((masks, w_phase, bias))
    mine = pick(arrived, masks, PICK_MINE)

    late = masks[LATE] > 0.5
    upper, lower = mine[0:7], mine[1:8]
    head, tail = mine[0:3], mine[5:8]
    quarter = range(4)
    rims = [
        lax.ppermute(
            jnp.where(late, lower, upper),
            "tile",
            [(s, 2 * s) for s in quarter] + [(4 + s, 2 * s + 1) for s in quarter],
        ),
        lax.ppermute(
            jnp.where(late, upper, lower),
            "tile",
            [(s, 2 * s + 1) for s in quarter] + [(4 + s, 2 * s) for s in quarter],
        ),
        lax.ppermute(
            jnp.where(late, tail, head),
            "tile",
            [(s, 2 * s - 1) for s in quarter if s > 0]
            + [(4 + s, 2 * s + 2) for s in quarter if s < 3],
        ),
        lax.ppermute(
            jnp.where(late, head, tail),
            "tile",
            [(s, 2 * s + 2) for s in quarter if s < 3]
            + [(4 + s, 2 * s - 1) for s in quarter if s > 0],
        ),
    ]
    weights = [
        bias,
        jnp.swapaxes(w_in, 3, 4).reshape(27 * LAT, MID),
        w_res.reshape(27, MID, MID),
        w_time,
        w_phase,
    ]
    return decode(masks, rims, weights)[None]


def solution(mesh):
    return jax.shard_map(
        on_device,
        mesh=mesh,
        in_specs=(P(("req", "tile"), None, None),) + (P(),) * 13,
        out_specs=P("req", None, None, "tile", None),
        check_vma=False,
    )
```
